512 devices in a mesh: outer: 8 (over x, y_lo), inner: 64 (over z, y_hi, core).
Axes of the slice: x: 4, y: 4 (y_hi: 2, y_lo: 2; y = y_hi * 2 + y_lo), z: 16, core: 2. Of those that a mesh axis runs over, the one named last changes fastest.
Arguments:
- queries: bfloat16 [16384, 2048], P('inner'), may hold values from -128 to 128
- mem_keys: bfloat16 [8192, 2048], P(('outer', 'inner')), may hold values from -4.5 to 4.5
- mem_values: bfloat16 [8192, 2048], P(('outer', 'inner')), may hold values from -6 to 6
Outputs:
- attended: bfloat16 [16384, 2048], P('inner')
- log_total: float32 [16384, 16], P('inner')
The draws below stay inside these ranges and needn't reach their ends.
All inputs are finite; a program needn't handle non-finite values.
Results may differ from the reference program's by a relative error of at most 0.014.
Values may be sent and summed in bfloat16 or wider, within the bound.
No kernel may reach another device: no remote copies, remote signals or barrier semaphores. Data moves between devices by JAX's collectives and lax.ppermute only.
A program may use at most 64 MiB of HBM per device.

```python
import math
import jax
import jax.numpy as jnp
from jax import lax

HEADS = 16
HEAD_DIM = 128
TOKENS = 16384
MEMORY = 8192
COLUMNS = 2048
N_OUTER = 8


def key_field(key):
    stream = jax.random.fold_in(key, 202)
    columns = HEADS * HEAD_DIM
    field = jnp.clip(jax.random.normal(stream, (MEMORY, columns), jnp.float32), -4.5, 4.5)
    return field.astype(jnp.bfloat16)


def draw_mem_keys(key, part):
    return key_field(key)


def draw_queries(key, part):
    stream = jax.random.fold_in(key, 303)
    columns = HEADS * HEAD_DIM
    field = 3.0 * jnp.clip(jax.random.normal(stream, (TOKENS, columns), jnp.float32), -6.0, 6.0)
    return field.astype(jnp.bfloat16)


def steps_of(stream_key, shape, cuts, low, high):
    def one(axis_at, parts):
        draws = jax.random.uniform(jax.random.fold_in(jax.random.fold_in(stream_key, 6), axis_at), (parts,), jnp.float32, low / len(cuts), high / len(cuts))
        return jnp.repeat(jnp.exp(draws), shape[axis_at] // parts).reshape((-1,) + (1,) * (len(shape) - axis_at - 1))

    factor_of = one(*cuts[0])
    for cut in cuts[1:]:
        factor_of = factor_of * one(*cut)
    return factor_of


def centred(key, shape, scale, bound, cuts=(), kind=jnp.bfloat16):
    entries = scale * jax.random.normal(key, shape, jnp.float32)
    if cuts:
        entries = entries * steps_of(key, shape, cuts, -0.22, 0.18)
    return jnp.clip(entries, -bound, bound).astype(kind)


def setup_inputs(seed: int = 0) -> dict:
    streams_of = jax.random.split(jax.random.key(seed), 4)
    return {
        "queries": draw_queries(jax.random.fold_in(streams_of[3], 71), 0),
        "mem_keys": draw_mem_keys(jax.random.fold_in(streams_of[3], 71), 0),
        "mem_values": centred(streams_of[2], (MEMORY, COLUMNS), 1.0, 6.0, ((0, 512),)),
    }


def reference(queries, mem_keys, mem_values):
    scale = 1.0 / math.sqrt(HEAD_DIM)
    per_group = MEMORY // N_OUTER
    key_groups = mem_keys.astype(jnp.float32).reshape(N_OUTER, per_group, HEADS, HEAD_DIM)
    value_groups = mem_values.astype(jnp.float32).reshape(N_OUTER, per_group, HEADS, HEAD_DIM)
    block_rows = math.gcd(TOKENS, 512)
    query_blocks = queries.astype(jnp.float32).reshape(TOKENS // block_rows, block_rows, HEADS, HEAD_DIM)

    def one_block(query_block):
        scores = jnp.einsum('thd,gkhd->thgk', query_block, key_groups) * scale
        group_peak = lax.optimization_barrier(jnp.max(scores, axis=-1))
        raw = jnp.exp(scores - group_peak[..., None])
        group_total = lax.optimization_barrier(jnp.sum(raw, axis=-1))
        weights = lax.optimization_barrier(raw.astype(jnp.bfloat16)).astype(jnp.float32)
        group_out = jnp.einsum('thgk,gkhd->thgd', weights, value_groups)
        peak = lax.optimization_barrier(jnp.max(group_peak, axis=-1))
        factor = jnp.exp(group_peak - peak[..., None])
        shares = lax.optimization_barrier((group_out * factor[..., None]).astype(jnp.bfloat16)).astype(jnp.float32)
        summed = lax.optimization_barrier(jnp.sum(shares, axis=2))
        total = lax.optimization_barrier(jnp.sum(group_total * factor, axis=-1))
        attended = (summed / total[..., None]).astype(jnp.bfloat16).reshape(block_rows, HEADS * HEAD_DIM)
        log_total = peak + jnp.log(total)
        return (attended, log_total)
    attended, log_total = lax.map(one_block, query_blocks)
    return (attended.reshape(TOKENS, HEADS * HEAD_DIM), log_total.reshape(TOKENS, HEADS))
```

```python
import functools
import math

import jax
import jax.numpy as jnp
from jax import lax
from jax.experimental import pallas as pl
from jax.experimental.pallas import tpu as pltpu
from jax.sharding import Mesh
from jax.sharding import PartitionSpec as P

HEADS = 16
DIM = 128
SCALE = 1.0 / math.sqrt(DIM)
TO_BASE_TWO = SCALE / math.log(2.0)

NAMES = ("x", "y_lo", "z", "y_hi", "core")
SIZES = (4, 2, 16, 2, 2)
OUTER = ("x", "y_lo")
INNER = ("z", "y_hi", "core")
PLANE = ("x", "y_lo", "y_hi")

OWN = 16
SHARE = 32
PEERS = 16
LINE = OWN * PEERS
TOKENS = SHARE * PEERS

VMEM = pltpu.VMEM


def whole(count):
    return [pl.BlockSpec(memory_space=VMEM)] * count


def pack_kernel(which, q_ref, k_ref, v_ref, out_ref):
    for head in range(HEADS):
        columns = slice(head * DIM, (head + 1) * DIM)
        out_ref[head, 0:OWN, :] = k_ref[:, columns]
        out_ref[head, OWN : 2 * OWN, :] = v_ref[:, columns]
        out_ref[head, 2 * OWN : 2 * OWN + SHARE, :] = q_ref[:, columns]


def pack(which, queries, keys, values):
    columns = HEADS * DIM
    grid_spec = pltpu.PrefetchScalarGridSpec(
        num_scalar_prefetch=1,
        grid=(1,),
        in_specs=[
            pl.BlockSpec((SHARE, columns), lambda i, w: (w[0], 0)),
            pl.BlockSpec((OWN, columns), lambda i, w: (0, 0)),
            pl.BlockSpec((OWN, columns), lambda i, w: (0, 0)),
        ],
        out_specs=pl.BlockSpec((HEADS, 2 * OWN + SHARE, DIM), lambda i, w: (0, 0, 0)),
    )
    return pl.pallas_call(
        pack_kernel,
        out_shape=jax.ShapeDtypeStruct((HEADS, 2 * OWN + SHARE, DIM), jnp.bfloat16),
        grid_spec=grid_spec,
        name="pack",
    )(which, queries, keys, values)


def spread_kernel(in_ref, kv_ref, q_ref):
    for peer in range(PEERS):
        for source in range(PEERS):
            rows = slice(source * OWN, (source + 1) * OWN)
            kv_ref[peer, rows, :] = in_ref[source, 0:OWN, :]
        for source in range(PEERS):
            rows = slice(LINE + source * OWN, LINE + (source + 1) * OWN)
            kv_ref[peer, rows, :] = in_ref[source, OWN : 2 * OWN, :]
    for source in range(PEERS):
        q_ref[source * SHARE : (source + 1) * SHARE, :] = in_ref[source, 2 * OWN :, :]


def spread(received):
    return pl.pallas_call(
        spread_kernel,
        out_shape=(
            jax.ShapeDtypeStruct((PEERS, 2 * LINE, DIM), jnp.bfloat16),
            jax.ShapeDtypeStruct((TOKENS, DIM), jnp.bfloat16),
        ),
        in_specs=whole(1),
        out_specs=tuple(whole(2)),
        name="spread",
    )(received)


T_BLOCK = 256
P_BLOCK = 4


def attend(q, kv_ref, first, state):
    keys = kv_ref[first : first + P_BLOCK, 0:LINE, :].reshape(P_BLOCK * LINE, DIM)
    values = kv_ref[first : first + P_BLOCK, LINE:, :].reshape(P_BLOCK * LINE, DIM)
    scores = lax.dot_general(
        q, keys, (((1,), (1,)), ((), ())), preferred_element_type=jnp.float32
    )
    top = jnp.max(scores, axis=1, keepdims=True)
    if state is not None:
        top = jnp.maximum(top, state[0])
    raw = jnp.exp2((scores - top) * TO_BASE_TWO)
    total = jnp.sum(raw, axis=1, keepdims=True)
    out = jnp.dot(raw.astype(jnp.bfloat16), values, preferred_element_type=jnp.float32)
    if state is not None:
        fading = jnp.exp2((state[0] - top) * TO_BASE_TWO)
        total = total + state[1] * fading
        out = out + state[2] * fading
    return top, total, out


def first_kernel(q_ref, kv_ref, top_ref, total_ref, out_ref):
    for block in range(TOKENS // T_BLOCK):
        rows = slice(block * T_BLOCK, (block + 1) * T_BLOCK)
        q = q_ref[rows, :]
        state = None
        for first in range(0, PEERS, P_BLOCK):
            state = attend(q, kv_ref, first, state)
        top_ref[rows, :] = jnp.broadcast_to(state[0], (T_BLOCK, DIM))
        total_ref[rows, :] = jnp.broadcast_to(state[1], (T_BLOCK, DIM))
        out_ref[rows, :] = state[2]


def second_kernel(q_ref, kv_ref, top_ref, total_ref, out_ref, packed_ref):
    for block in range(TOKENS // T_BLOCK):
        rows = slice(block * T_BLOCK, (block + 1) * T_BLOCK)
        q = q_ref[rows, :]
        state = (top_ref[rows, 0:1], total_ref[rows, 0:1], out_ref[rows, :])
        for first in range(0, PEERS, P_BLOCK):
            state = attend(q, kv_ref, first, state)
        top, total, out = state
        packed_ref[rows, 0:DIM] = (out / total).astype(jnp.bfloat16)
        log_total = top * SCALE + jnp.log(total)
        high = log_total.astype(jnp.bfloat16)
        low = (log_total - high.astype(jnp.float32)).astype(jnp.bfloat16)
        lane = lax.broadcasted_iota(jnp.int32, (T_BLOCK, DIM), 1)
        packed_ref[rows, DIM:] = jnp.where(
            lane < HEADS, high.astype(jnp.float32), low.astype(jnp.float32)
        ).astype(jnp.bfloat16)


COST = pl.CostEstimate(
    flops=4 * TOKENS * PEERS * LINE * DIM,
    bytes_accessed=2 * PEERS * 2 * LINE * DIM,
    transcendentals=TOKENS * PEERS * LINE,
)


def flash_first(q, kv):
    return pl.pallas_call(
        first_kernel,
        out_shape=(jax.ShapeDtypeStruct((TOKENS, DIM), jnp.float32),) * 3,
        in_specs=whole(2),
        out_specs=tuple(whole(3)),
        cost_estimate=COST,
        name="first_half",
    )(q, kv)


def flash_second(q, kv, state):
    return pl.pallas_call(
        second_kernel,
        out_shape=jax.ShapeDtypeStruct((TOKENS, 2 * DIM), jnp.bfloat16),
        in_specs=whole(5),
        out_specs=whole(1)[0],
        cost_estimate=COST,
        name="second_half",
    )(q, kv, *state)


N_OUTER = 8
WIDE = HEADS * DIM + DIM


def gather_kernel(in_ref, out_ref):
    lane = lax.broadcasted_iota(jnp.int32, (SHARE, DIM), 1)
    logs = jnp.zeros((SHARE, DIM), jnp.float32)
    for head in range(HEADS):
        here = in_ref[head, :, DIM:].astype(jnp.float32)
        logs = jnp.where((lane == head) | (lane == HEADS + head), here, logs)
    logs = logs.astype(jnp.bfloat16)
    for copy in range(N_OUTER):
        for head in range(HEADS):
            out_ref[copy, :, head * DIM : (head + 1) * DIM] = in_ref[head, :, 0:DIM]
        out_ref[copy, :, HEADS * DIM :] = logs


def widen(received):
    return pl.pallas_call(
        gather_kernel,
        out_shape=jax.ShapeDtypeStruct((N_OUTER, SHARE, WIDE), jnp.bfloat16),
        in_specs=whole(1),
        out_specs=whole(1)[0],
        name="widen",
    )(received)


def finish_kernel(in_ref, attended_ref, log_ref):
    for source in range(N_OUTER):
        rows = slice(source * SHARE, (source + 1) * SHARE)
        attended_ref[rows, :] = in_ref[source, :, 0 : HEADS * DIM]
        logs = in_ref[source, :, HEADS * DIM :].astype(jnp.float32)
        log_ref[rows, :] = logs[:, 0:HEADS] + logs[:, HEADS : 2 * HEADS]


def finish(received):
    rows = N_OUTER * SHARE
    return pl.pallas_call(
        finish_kernel,
        out_shape=(
            jax.ShapeDtypeStruct((rows, HEADS * DIM), jnp.bfloat16),
            jax.ShapeDtypeStruct((rows, HEADS), jnp.float32),
        ),
        in_specs=whole(1),
        out_specs=tuple(whole(2)),
        name="finish",
    )(received)


def on_device(queries, mem_keys, mem_values):
    which = lax.axis_index(OUTER).astype(jnp.int32).reshape(1)
    packed = pack(which, queries, mem_keys, mem_values)
    received = lax.all_to_all(packed, "z", 0, 0)
    spread_out, q = spread(received)
    own = lax.all_to_all(spread_out, PLANE, 0, 0)
    other = lax.ppermute(own, "core", [(0, 1), (1, 0)])
    state = flash_first(q, own)
    result = flash_second(q, other, state)
    back = lax.all_to_all(result.reshape(PEERS, SHARE, 2 * DIM), "z", 0, 0)
    full = lax.all_to_all(widen(back), OUTER, 0, 0)
    return finish(full)


def solution(mesh):
    named = Mesh(mesh.devices.reshape(SIZES), NAMES)
    in_specs = (P(INNER, None), P(OUTER + INNER, None), P(OUTER + INNER, None))
    out_specs = (P(INNER, None), P(INNER, None))
    return jax.shard_map(
        on_device, mesh=named, in_specs=in_specs, out_specs=out_specs, check_vma=False
    )
```
